32 devices in a mesh: grp: 2 (over x), depth: 8 (over z, y), shot: 2 (over core).
Axes of the slice: x: 2, y: 2, z: 4, core: 2. Of those that a mesh axis runs over, the one named last changes fastest.
Arguments:
- src_now: float32 [4, 64, 128, 128], P(('grp', 'shot'), 'depth'), parts along dimension 0, may hold values from -6 to 6
- src_prev: float32 [4, 64, 128, 128], P(('grp', 'shot'), 'depth'), parts along dimension 0, may hold values from -6 to 6
- rcv_now: float32 [4, 64, 128, 128], P(('grp', 'shot'), 'depth'), parts along dimension 0, may hold values from -6 to 6
- rcv_prev: float32 [4, 64, 128, 128], P(('grp', 'shot'), 'depth'), parts along dimension 0, may hold values from -6 to 6
- courant_sq: float32 [128, 128, 128], P(('grp', 'depth')), parts along dimension 0, may hold values from 0.03 to 0.2
- source_cells: int32 [64], replicated, may hold values from 0 to 1048575
- shot_signs: int32 [4, 64], P(('grp', 'shot')), parts along dimension 0, may hold values from 0 to 1
- source_wavelet: float32 [3, 64], replicated, may hold values from -40 to 40
- receiver_cells: int32 [64], replicated, may hold values from 0 to 1048575
- receiver_data: float32 [4, 3, 64], P(('grp', 'shot')), parts along dimension 0, may hold values from -40 to 40
- wedge_bin: int32 [64, 128], P('shot'), may hold values from 0 to 15
- wedge_weight: float32 [16], replicated, may hold values from 0.2 to 2
- shrink_level: float32 [16], replicated, may hold values from 0.3 to 3
Outputs:
- shrunk_real: float32 [256, 64, 128], P(('grp', 'depth'), 'shot'), parts along dimension 0
- shrunk_imag: float32 [256, 64, 128], P(('grp', 'depth'), 'shot'), parts along dimension 0
The draws below stay inside these ranges and needn't reach their ends.
There are 2 independent parts, one for each index of `grp`. The reference program is written for one: setup_inputs(seed, part) draws one part's arguments, and reference() takes and returns one part's arrays. A program takes and returns all parts, laid end to end along the dimension named above; an argument that names none is the same for every part. Nothing has to cross between parts.
All inputs are finite; a program needn't handle non-finite values.
Results may differ from the reference program's by a relative error of at most 0.0001.
Values sent between devices are 32-bit elements; how exact they have to be, the bound alone decides.
A program may use at most 128 MiB of HBM per device.

```python
import math
import jax
import jax.numpy as jnp
from jax import lax

NY = 128
NZ = 128
STEPS = 3
NSRC = 64
NREC = 64
NBINS = 16
NX = 64
SHOTS = 2


def plant(drawn, own_key, low, top_value):
    longest = drawn.shape.index(max(drawn.shape))
    spots = []
    for shift in (0, 1):
        where = [jax.random.randint(jax.random.fold_in(own_key, axis), (), 0, length) for axis, length in enumerate(drawn.shape)]
        where[longest] = (where[longest] + shift) % drawn.shape[longest]
        spots.append(tuple(where))
    return drawn.at[spots[0]].set(low).at[spots[1]].set(top_value)


def level_of(own_key, dims, shards, low, largest):
    loudness = 1.0
    for axis_at, parts in shards:
        heights = jax.random.uniform(jax.random.fold_in(jax.random.fold_in(own_key, 6), axis_at), (parts,), jnp.float32, low / len(shards), largest / len(shards))
        loudness = loudness * jnp.repeat(jnp.exp(heights), dims[axis_at] // parts).reshape((-1,) + (1,) * (len(dims) - 1 - axis_at))
    return loudness


def centred(stream_key, shape, deviation, most, split=(), kind=jnp.bfloat16):
    entries = jax.random.normal(stream_key, shape, jnp.float32) * deviation
    if len(split) > 0:
        entries = level_of(stream_key, shape, split, -0.22, 0.18) * entries
    return jnp.clip(entries, min=-most, max=most).astype(kind)


def setup_inputs(seed: int = 0, part: int = 0) -> dict:
    seeds = jax.random.split(jax.random.key(seed), 14)
    part_keys = jax.random.split(jax.random.fold_in(seeds[13], part), 14)
    src_now = centred(part_keys[0], (SHOTS, NX, NY, NZ), 1.0, 6.0, ((0, 2), (1, 8)), jnp.float32)
    src_prev = centred(part_keys[1], (SHOTS, NX, NY, NZ), 1.0, 6.0, ((0, 2), (1, 8)), jnp.float32)
    rcv_now = centred(part_keys[2], (SHOTS, NX, NY, NZ), 1.0, 6.0, ((0, 2), (1, 8)), jnp.float32)
    rcv_prev = centred(part_keys[3], (SHOTS, NX, NY, NZ), 1.0, 6.0, ((0, 2), (1, 8)), jnp.float32)
    courant_sq = jnp.clip(jnp.exp(math.log(0.2) - 1.89712 * jax.random.uniform(part_keys[4], (NX, NY, NZ), jnp.float32) ** level_of(part_keys[4], (NX, NY, NZ), ((0, 8),), -0.2, 0.2)), 0.03, 0.2)
    source_cells = plant(jax.random.randint(seeds[5], (NSRC,), 0, NX * NY * NZ), jax.random.fold_in(seeds[5], 1), 0, (NX * NY * NZ) - 1).astype(jnp.int32)
    shot_signs = plant(jax.random.randint(part_keys[6], (SHOTS, NSRC), 0, 2), jax.random.fold_in(part_keys[6], 1), 0, 1).astype(jnp.int32)
    source_wavelet = centred(seeds[7], (STEPS, NSRC), 8.0, 40.0, (), jnp.float32)
    receiver_cells = plant(jax.random.randint(seeds[8], (NREC,), 0, NX * NY * NZ), jax.random.fold_in(seeds[8], 1), 0, (NX * NY * NZ) - 1).astype(jnp.int32)
    receiver_data = centred(part_keys[9], (SHOTS, STEPS, NREC), 8.0, 40.0, ((0, 2),), jnp.float32)
    wedge_bin = plant(jax.random.randint(seeds[10], (NX, NY), 0, NBINS), jax.random.fold_in(seeds[10], 1), 0, NBINS - 1).astype(jnp.int32)
    wedge_weight = jnp.clip(jnp.exp(jax.random.uniform(seeds[11], (NBINS,), jnp.float32, math.log(0.2), math.log(2.0))), 0.2, 2.0)
    shrink_level = jnp.clip(jnp.exp(jax.random.uniform(seeds[12], (NBINS,), jnp.float32, math.log(0.3), math.log(3.0))), 0.3, 3.0)
    return dict(src_now=src_now, src_prev=src_prev, rcv_now=rcv_now, rcv_prev=rcv_prev, courant_sq=courant_sq, source_cells=source_cells, shot_signs=shot_signs, source_wavelet=source_wavelet, receiver_cells=receiver_cells, receiver_data=receiver_data, wedge_bin=wedge_bin, wedge_weight=wedge_weight, shrink_level=shrink_level)


CENTER = -2.5
NEAR = 4.0 / 3.0
FAR = -1.0 / 12.0

def shifted(field, offset, axis):
    length = field.shape[axis]
    widths = [(0, 0)] * field.ndim
    if offset > 0:
        part = lax.slice_in_dim(field, offset, length, axis=axis)
        widths[axis] = (0, offset)
    else:
        part = lax.slice_in_dim(field, 0, length + offset, axis=axis)
        widths[axis] = (-offset, 0)
    return jnp.pad(part, widths)

def laplace(field):
    total = 3.0 * CENTER * field
    for axis in (1, 2, 3):
        total = total + NEAR * (shifted(field, 1, axis) + shifted(field, -1, axis))
        total = total + FAR * (shifted(field, 2, axis) + shifted(field, -2, axis))
    return total

def inject(flat_cells, amplitude):
    depth_idx = (flat_cells // (NY * NZ)).astype(jnp.int32)
    cross_idx = (flat_cells // NZ % NY).astype(jnp.int32)
    inline_idx = (flat_cells % NZ).astype(jnp.int32)
    empty = jnp.zeros((SHOTS, NX, NY, NZ), jnp.float32)
    return empty.at[:, depth_idx, cross_idx, inline_idx].add(amplitude)

def reference(src_now, src_prev, rcv_now, rcv_prev, courant_sq, source_cells, shot_signs, source_wavelet, receiver_cells, receiver_data, wedge_bin, wedge_weight, shrink_level):
    signs = (2 * shot_signs - 1).astype(jnp.float32)
    image = jnp.zeros((NX, NY, NZ), jnp.float32)
    for step in range(STEPS):
        src_next = 2.0 * src_now - src_prev + courant_sq[None] * laplace(src_now) + inject(source_cells, signs * source_wavelet[step][None, :])
        rcv_next = 2.0 * rcv_now - rcv_prev + courant_sq[None] * laplace(rcv_now) + inject(receiver_cells, receiver_data[:, STEPS - 1 - step, :])
        image = image + lax.optimization_barrier(jnp.sum(src_next * rcv_next, axis=0))
        src_prev, src_now = (src_now, src_next)
        rcv_prev, rcv_now = (rcv_now, rcv_next)
    spectrum = jnp.fft.fftn(image, norm='ortho')
    spec_re = jnp.transpose(jnp.real(spectrum), (2, 0, 1))
    spec_im = jnp.transpose(jnp.imag(spectrum), (2, 0, 1))
    weight = wedge_weight[wedge_bin][None]
    level = shrink_level[wedge_bin][None]
    real_part = weight * spec_re
    imag_part = weight * spec_im
    factor = 1.0 - level / jnp.sqrt(real_part * real_part + imag_part * imag_part + level * level)
    return ((factor * real_part).astype(jnp.float32), (factor * imag_part).astype(jnp.float32))
```

```python
import functools
import math

import jax
import jax.numpy as jnp
import numpy as np
from jax import lax
from jax.experimental import pallas as pl
from jax.experimental.pallas import tpu as pltpu
from jax.sharding import PartitionSpec as P

CENTER = -2.5
NEAR = 4.0 / 3.0
FAR = -1.0 / 12.0
MESH = pl.DeviceIdType.MESH
BF = jnp.bfloat16
F32 = jnp.float32


def dft_pair(length):
    index = np.arange(length)
    angle = (index[:, None] * index[None, :] % length) * (2.0 * math.pi / length)
    scale = 1.0 / math.sqrt(length)
    return np.cos(angle) * scale, np.sin(angle) * scale


def halves(table):
    table = table.astype(np.float32)
    high = table.astype(BF)
    low = (table - high.astype(np.float32)).astype(BF)
    return high, low


def split(value):
    high = value.astype(BF)
    return high, (value - high.astype(F32)).astype(BF)


def dot(a, b, dims):
    return lax.dot_general(a, b, (dims, ((), ())), preferred_element_type=F32)


def dot3(a, b, dims):
    (ah, al), (bh, bl) = a, b
    return dot(ah, bh, dims) + (dot(ah, bl, dims) + dot(al, bh, dims))


NN = ((1,), (0,))
NT = ((1,), (1,))


def kernel(
    nd, ns, steps, rows, cross, inline, bins, sizes,
    sn, sp, rn, rp, cs, scell, ssign, swave, rcell, rdata, wbin, wweight, slevel,
    tzh, tzl, tyh, tyl, txh, txl,
    out_re, out_im,
    halo, waves, image, arrived, send, recv, xh, xl, swap_out, swap_in,
    halo_send, halo_recv, shot_sems, all_send, all_recv, swap_sems,
):
    depth_len, half, kzs = sizes
    g, d, s = lax.axis_index("grp"), lax.axis_index("depth"), lax.axis_index("shot")
    n = nd * ns
    me = d * ns + s
    block = half * 2 * kzs

    def at(j):
        return (g, j // ns, lax.rem(j, ns))

    barrier = pltpu.get_barrier_semaphore()

    def greet(o, carry):
        pl.semaphore_signal(
            barrier, inc=1, device_id=at(lax.rem(me + o, n)), device_id_type=MESH
        )
        return carry

    lax.fori_loop(1, n, greet, 0)
    pl.semaphore_wait(barrier, n - 1)

    now = [[sn.at[0], rn.at[0]]] + [[waves.at[t, 0], waves.at[t, 1]] for t in range(steps - 1)]
    before = [[sp.at[0], rp.at[0]]] + now

    def halo_copy(t, way, f):
        rows_from = now[t][f].at[pl.ds(0 if way == 0 else rows - 2, 2)]
        return pltpu.make_async_remote_copy(
            src_ref=rows_from,
            dst_ref=halo.at[t, way, f],
            send_sem=halo_send.at[t, way, f],
            recv_sem=halo_recv.at[t, way, f],
            device_id=(g, d - 1 if way == 0 else d + 1, s),
            device_id_type=MESH,
        )

    has = (d > 0, d < nd - 1)

    def halos(t, act, flip):
        for way in (0, 1):
            @pl.when(has[1 - way if flip else way])
            def _():
                for f in (0, 1):
                    getattr(halo_copy(t, way, f), act)()

    halos(0, "start", False)

    for way in (0, 1):
        @pl.when(jnp.logical_not(has[1 - way]))
        def _():
            for t in range(steps):
                for f in (0, 1):
                    halo[t, way, f] = jnp.zeros((2, cross, inline), F32)

    row_iota = lax.broadcasted_iota(jnp.int32, (cross, 1), 0)
    lane = lax.broadcasted_iota(jnp.int32, (1, inline), 1)
    twice = lambda v: jnp.concatenate([v, v], axis=1)
    place = []
    for cells in (scell, rcell):
        c = twice(cells[...])
        depth_idx = c // (cross * inline)
        cross_idx = lax.rem(c // inline, cross)
        inline_idx = lax.rem(c, inline)
        on_y = row_iota == cross_idx
        zt = lax.broadcasted_iota(jnp.int32, (inline, 1), 0) == inline_idx
        place.append((depth_idx, on_y, jnp.where(zt, 1.0, 0.0).astype(BF)))
    signs = (2 * ssign[...] - 1).astype(F32)

    def amplitude(t, f):
        if f == 0:
            amp = signs * swave[pl.ds(t, 1), :]
        else:
            amp = rdata[0, pl.ds(steps - 1 - t, 1), :]
        high = amp.astype(BF).astype(F32)
        return jnp.concatenate([high, amp - high], axis=1)

    def forcing(amp, f, r):
        depth_idx, on_y, zt = place[f]
        amp_row = jnp.where(depth_idx == d * rows + r, amp, 0.0)
        left = jnp.where(on_y, amp_row, 0.0).astype(BF)
        return dot(left, zt, NT)

    lane_coef = [
        (k, jnp.where((lane + k >= 0) & (lane + k < inline), c, 0.0))
        for k, c in ((1, NEAR), (-1, NEAR), (2, FAR), (-2, FAR))
    ]

    def move(u, k):
        zero = jnp.zeros((abs(k), inline), F32)
        if k > 0:
            return jnp.concatenate([u[k:], zero], axis=0)
        return jnp.concatenate([zero, u[:k]], axis=0)

    def advance(t, r, amps):
        result = []
        for f in (0, 1):
            field = now[t][f]

            def layer(q):
                if q < 0:
                    return halo[t, 1, f, q + 2]
                if q >= rows:
                    return halo[t, 0, f, q - rows]
                return field[q]

            u = layer(r)
            near = layer(r - 1) + layer(r + 1) + move(u, 1) + move(u, -1)
            far = layer(r - 2) + layer(r + 2) + move(u, 2) + move(u, -2)
            total = 3.0 * CENTER * u + NEAR * near + FAR * far
            for k, coef in lane_coef:
                total = total + coef * pltpu.roll(u, (-k) % inline, 1)
            new = 2.0 * u - before[t][f][r] + cs[r] * total + forcing(amps[f], f, r)
            if t < steps - 1:
                waves[t, f, r] = new
            result.append(new)
        product = result[0] * result[1]
        if t == 0:
            image[r] = product
        else:
            image[r] = image[r] + product

    for t in range(steps):
        amps = [amplitude(t, f) for f in (0, 1)]
        for r in range(2, rows - 2):
            advance(t, r, amps)
        halos(t, "wait_recv", True)
        for r in (0, 1, rows - 2, rows - 1):
            advance(t, r, amps)
        if t < steps - 1:
            halos(t + 1, "start", False)

    shot_copy = pltpu.make_async_remote_copy(
        src_ref=image.at[pl.ds((1 - s) * half, half)],
        dst_ref=arrived,
        send_sem=shot_sems.at[0],
        recv_sem=shot_sems.at[1],
        device_id=(g, d, 1 - s),
        device_id_type=MESH,
    )
    shot_copy.start()
    bin_map = wbin[...]
    weight = jnp.zeros(bin_map.shape, F32)
    level = jnp.zeros(bin_map.shape, F32)
    for b in range(bins):
        hit = bin_map == b
        weight = jnp.where(hit, wweight[b], weight)
        level = jnp.where(hit, slevel[b], level)
    shot_copy.wait_recv()

    tz = (tzh[...], tzl[...])
    ty = (tyh[...], tyl[...])
    for x in range(half):
        summed = image[s * half + x] + arrived[x]
        lines = dot3(tz, split(summed), NT)
        pair = jnp.concatenate([lines[:inline], lines[inline:]], axis=1)
        planes = dot3(split(pair), ty, NN)
        for p in (0, 1):
            plane = planes[:, p * cross : (p + 1) * cross]
            spot = (x * 2 + p) * kzs
            if kzs % 8 == 0:
                send[:, pl.ds(spot, kzs), :] = plane.reshape(n, kzs, cross)
            else:
                plane = plane.reshape(n, kzs, cross)
                for k in range(kzs):
                    send[:, spot + k, :] = plane[:, k]

    def exchange(o):
        other = lax.rem(me + o, n)
        return pltpu.make_async_remote_copy(
            src_ref=send.at[other],
            dst_ref=recv.at[pl.ds(pl.multiple_of(me * block, block), block)],
            send_sem=all_send.at[o],
            recv_sem=all_recv.at[o],
            device_id=at(other),
            device_id_type=MESH,
        )

    def start_one(o, carry):
        exchange(o).start()
        return carry

    lax.fori_loop(1, n, start_one, 0)
    recv[pl.ds(pl.multiple_of(me * block, block), block)] = send[me]

    def receive_one(o, carry):
        other = lax.rem(me + n - o, n)
        pltpu.make_async_remote_copy(
            src_ref=send.at[other],
            dst_ref=recv.at[pl.ds(pl.multiple_of(other * block, block), block)],
            send_sem=all_send.at[o],
            recv_sem=all_recv.at[o],
            device_id=at(other),
            device_id_type=MESH,
        ).wait_recv()
        return carry

    lax.fori_loop(1, n, receive_one, 0)

    for k in range(kzs):
        for p in (0, 1):
            part = recv[pl.ds(p * kzs + k, depth_len, stride=2 * kzs), :]
            high, low = split(part)
            spot = (pl.ds(p * depth_len, depth_len), pl.ds(k * cross, cross))
            xh[spot] = high
            xl[spot] = low

    width = depth_len // ns
    full = dot3((txh[1 - s], txl[1 - s]), (xh[...], xl[...]), NN)
    for p in (0, 1):
        for k in range(kzs):
            swap_out[p, k] = full[p * width : (p + 1) * width, k * cross : (k + 1) * cross]
    swap = pltpu.make_async_remote_copy(
        src_ref=swap_out,
        dst_ref=swap_in,
        send_sem=swap_sems.at[0],
        recv_sem=swap_sems.at[1],
        device_id=(g, d, 1 - s),
        device_id_type=MESH,
    )
    swap.start()

    def shrink(real, imag, spot):
        real, imag = weight * real, weight * imag
        factor = 1.0 - level * lax.rsqrt(real * real + imag * imag + level * level)
        out_re[spot] = factor * real
        out_im[spot] = factor * imag

    full = dot3((txh[s], txl[s]), (xh[...], xl[...]), NN)
    for k in range(kzs):
        lanes = slice(k * cross, (k + 1) * cross)
        shrink(full[:width, lanes], full[width:, lanes], s * kzs + k)
    swap.wait_recv()
    for k in range(kzs):
        shrink(swap_in[0, k], swap_in[1, k], (1 - s) * kzs + k)

    for t in range(steps):
        halos(t, "wait_send", False)
    shot_copy.wait_send()

    def sent_one(o, carry):
        exchange(o).wait_send()
        return carry

    lax.fori_loop(1, n, sent_one, 0)
    swap.wait_send()


def per_device(
    nd, ns,
    src_now, src_prev, rcv_now, rcv_prev, courant_sq, source_cells, shot_signs,
    source_wavelet, receiver_cells, receiver_data, wedge_bin, wedge_weight, shrink_level,
):
    _, rows, cross, inline = src_now.shape
    steps = source_wavelet.shape[0]
    n = nd * ns
    depth_len = rows * nd
    half = rows // ns
    kzs = inline // n
    block = half * 2 * kzs
    width = depth_len // ns
    c, s_ = dft_pair(inline)
    tz = halves(np.concatenate([c, -s_], axis=0))
    c, s_ = dft_pair(cross)
    ty = halves(np.block([[c, -s_], [s_, c]]))
    c, s_ = dft_pair(depth_len)
    tx = halves(
        np.stack(
            [
                np.block(
                    [
                        [c[h * width : (h + 1) * width], s_[h * width : (h + 1) * width]],
                        [-s_[h * width : (h + 1) * width], c[h * width : (h + 1) * width]],
                    ]
                )
                for h in range(ns)
            ]
        )
    )
    vmem = pl.BlockSpec(memory_space=pltpu.VMEM)
    smem = pl.BlockSpec(memory_space=pltpu.SMEM)
    out = jax.ShapeDtypeStruct((inline // nd, width, cross), F32)
    dma = pltpu.SemaphoreType.DMA
    return pl.pallas_call(
        functools.partial(
            kernel, nd, ns, steps, rows, cross, inline, wedge_weight.shape[0],
            (depth_len, half, kzs),
        ),
        out_shape=(out, out),
        in_specs=[vmem] * 11 + [smem] * 2 + [vmem] * 6,
        out_specs=(vmem, vmem),
        scratch_shapes=[
            pltpu.VMEM((steps, 2, 2, 2, cross, inline), F32),
            pltpu.VMEM((steps - 1, 2, rows, cross, inline), F32),
            pltpu.VMEM((rows, cross, inline), F32),
            pltpu.VMEM((half, cross, inline), F32),
            pltpu.VMEM((n, block, cross), F32),
            pltpu.VMEM((n * block, cross), F32),
            pltpu.VMEM((2 * depth_len, kzs * cross), BF),
            pltpu.VMEM((2 * depth_len, kzs * cross), BF),
            pltpu.VMEM((2, kzs, width, cross), F32),
            pltpu.VMEM((2, kzs, width, cross), F32),
            dma((steps, 2, 2)),
            dma((steps, 2, 2)),
            dma((2,)),
            dma((n,)),
            dma((n,)),
            dma((2,)),
        ],
        compiler_params=pltpu.CompilerParams(
            collective_id=0, has_side_effects=True, vmem_limit_bytes=56 * 1024 * 1024
        ),
    )(
        src_now, src_prev, rcv_now, rcv_prev, courant_sq,
        source_cells[None], shot_signs, source_wavelet, receiver_cells[None], receiver_data,
        wedge_bin, wedge_weight, shrink_level,
        *tz, *ty, *tx,
    )


def solution(mesh):
    return jax.shard_map(
        functools.partial(per_device, mesh.shape["depth"], mesh.shape["shot"]),
        mesh=mesh,
        in_specs=(
            P(("grp", "shot"), "depth", None, None),
            P(("grp", "shot"), "depth", None, None),
            P(("grp", "shot"), "depth", None, None),
            P(("grp", "shot"), "depth", None, None),
            P(("grp", "depth"), None, None),
            P(),
            P(("grp", "shot"), None),
            P(),
            P(),
            P(("grp", "shot"), None, None),
            P("shot", None),
            P(),
            P(),
        ),
        out_specs=(P(("grp", "depth"), "shot", None), P(("grp", "depth"), "shot", None)),
        check_vma=False,
    )
```

```python
import functools
import math

import jax
import jax.numpy as jnp
import numpy as np
from jax import lax
from jax.experimental import pallas as pl
from jax.experimental.pallas import tpu as pltpu
from jax.sharding import PartitionSpec as P

CENTER = -2.5
NEAR = 4.0 / 3.0
FAR = -1.0 / 12.0
MESH = pl.DeviceIdType.MESH
BF = jnp.bfloat16
F32 = jnp.float32


def dft_pair(length):
    index = np.arange(length)
    angle = (index[:, None] * index[None, :] % length) * (2.0 * math.pi / length)
    scale = 1.0 / math.sqrt(length)
    return np.cos(angle) * scale, np.sin(angle) * scale


def halves(table):
    table = table.astype(np.float32)
    high = table.astype(BF)
    low = (table - high.astype(np.float32)).astype(BF)
    return high, low


def split(value):
    high = value.astype(BF)
    return high, (value - high.astype(F32)).astype(BF)


def dot(a, b, dims):
    return lax.dot_general(a, b, (dims, ((), ())), preferred_element_type=F32)


def dot3(a, b, dims):
    (ah, al), (bh, bl) = a, b
    return dot(ah, bh, dims) + (dot(ah, bl, dims) + dot(al, bh, dims))


NN = ((1,), (0,))
NT = ((1,), (1,))


def phase_start(counts, half, rows, phase, core):
    if len(counts) == 1:
        return core * half
    if phase == 0:
        return 2 + core * (half - 2)
    return core * (rows - 2)


def kernel(
    nd, ns, steps, rows, cross, inline, bins, sizes,
    sn, sp, rn, rp, cs, scell, ssign, swave, rcell, rdata, wbin, wweight, slevel,
    tzh, tzl, tyh, tyl, txh, txl,
    out_re, out_im,
    staged, courant, halo, waves, image, xh, xl, swap_out, swap_in,
    halo_send, halo_recv, shot_sems, all_send, all_recv, swap_sems, stage_sems,
    *buffers,
):
    depth_len, half, kzs, counts = sizes
    phases = len(counts)
    arrived, send, recv = (buffers[i * phases : (i + 1) * phases] for i in range(3))
    g, d, s = lax.axis_index("grp"), lax.axis_index("depth"), lax.axis_index("shot")
    n = nd * ns
    me = d * ns + s

    def rows_at(phase, core):
        return phase_start(counts, half, rows, phase, core)

    def at(j):
        return (g, j // ns, lax.rem(j, ns))

    stages = [
        pltpu.make_async_copy(src, dst, stage_sems.at[i])
        for i, (src, dst) in enumerate(
            [
                (sn.at[0], staged.at[0]),
                (sp.at[0], staged.at[1]),
                (cs, courant),
                (rn.at[0], staged.at[2]),
                (rp.at[0], staged.at[3]),
            ]
        )
    ]
    for stage in stages:
        stage.start()
    barrier = pltpu.get_barrier_semaphore()

    def greet(o, carry):
        pl.semaphore_signal(
            barrier, inc=1, device_id=at(lax.rem(me + o, n)), device_id_type=MESH
        )
        return carry

    lax.fori_loop(1, n, greet, 0)
    pl.semaphore_wait(barrier, n - 1)

    now = [[staged.at[0], staged.at[2]]] + [[waves.at[t, 0], waves.at[t, 1]] for t in range(steps)]
    before = [[staged.at[1], staged.at[3]]] + now
    outgoing = [[sn.at[0], rn.at[0]]] + now[1:]

    def halo_copy(t, way, f):
        rows_from = outgoing[t][f].at[pl.ds(0 if way == 0 else rows - 2, 2)]
        return pltpu.make_async_remote_copy(
            src_ref=rows_from,
            dst_ref=halo.at[t, way, f],
            send_sem=halo_send.at[t, way, f],
            recv_sem=halo_recv.at[t, way, f],
            device_id=(g, d - 1 if way == 0 else d + 1, s),
            device_id_type=MESH,
        )

    has = (d > 0, d < nd - 1)

    def halo_send_do(t, way, f, act):
        @pl.when(has[way])
        def _():
            getattr(halo_copy(t, way, f), act)()

    def halo_wait(t, way, f):
        @pl.when(has[1 - way])
        def _():
            halo_copy(t, way, f).wait_recv()

    for f in (0, 1):
        for way in (0, 1):
            halo_send_do(0, way, f, "start")

    for way in (0, 1):
        @pl.when(jnp.logical_not(has[1 - way]))
        def _():
            for t in range(steps):
                for f in (0, 1):
                    halo[t, way, f] = jnp.zeros((2, cross, inline), F32)

    row_iota = lax.broadcasted_iota(jnp.int32, (cross, 1), 0)
    lane = lax.broadcasted_iota(jnp.int32, (1, inline), 1)
    twice = lambda v: jnp.concatenate([v, v], axis=1)
    place = []
    for cells in (scell, rcell):
        c = twice(cells[...])
        depth_idx = c // (cross * inline)
        cross_idx = lax.rem(c // inline, cross)
        inline_idx = lax.rem(c, inline)
        on_y = row_iota == cross_idx
        zt = lax.broadcasted_iota(jnp.int32, (inline, 1), 0) == inline_idx
        place.append((depth_idx, on_y, jnp.where(zt, 1.0, 0.0).astype(BF)))
    signs = (2 * ssign[...] - 1).astype(F32)

    def amplitude(t, f):
        if f == 0:
            amp = signs * swave[pl.ds(t, 1), :]
        else:
            amp = rdata[steps - 1 - t]
        high = amp.astype(BF).astype(F32)
        return jnp.concatenate([high, amp - high], axis=1)

    def forcing(amp, f, r):
        depth_idx, on_y, zt = place[f]
        amp_row = jnp.where(depth_idx == d * rows + r, amp, 0.0)
        left = jnp.where(on_y, amp_row, 0.0).astype(BF)
        return dot(left, zt, NT)

    lane_coef = [
        (k, jnp.where((lane + k >= 0) & (lane + k < inline), c, 0.0))
        for k, c in ((1, NEAR), (-1, NEAR), (2, FAR), (-2, FAR))
    ]

    def move(u, k):
        zero = jnp.zeros((abs(k), inline), F32)
        if k > 0:
            return jnp.concatenate([u[k:], zero], axis=0)
        return jnp.concatenate([zero, u[:k]], axis=0)

    def advance(t, f, r, amp):
        field = now[t][f]

        def layer(q):
            if q < 0:
                return halo[t, 1, f, q + 2]
            if q >= rows:
                return halo[t, 0, f, q - rows]
            return field[q]

        u = layer(r)
        near = layer(r - 1) + layer(r + 1) + move(u, 1) + move(u, -1)
        far = layer(r - 2) + layer(r + 2) + move(u, 2) + move(u, -2)
        total = 3.0 * CENTER * u + NEAR * near + FAR * far
        for k, coef in lane_coef:
            total = total + coef * pltpu.roll(u, (-k) % inline, 1)
        new = 2.0 * u - before[t][f][r] + courant[r] * total + forcing(amp, f, r)
        if t < steps - 1 or f == 0:
            waves[t, f, r] = new
        if f == 1:
            product = waves[t, 0, r] * new
            if t == 0:
                image[r] = product
            else:
                image[r] = image[r] + product

    def shot_copy(phase):
        return pltpu.make_async_remote_copy(
            src_ref=image.at[pl.ds(rows_at(phase, 1 - s), counts[phase])],
            dst_ref=arrived[phase],
            send_sem=shot_sems.at[phase, 0],
            recv_sem=shot_sems.at[phase, 1],
            device_id=(g, d, 1 - s),
            device_id_type=MESH,
        )

    tz = (tzh[...], tzl[...])
    ty = (tyh[...], tyl[...])

    def transform(phase):
        mine = rows_at(phase, s)
        for x in range(counts[phase]):
            summed = image[mine + x] + arrived[phase][x]
            lines = dot3(tz, split(summed), NT)
            pair = jnp.concatenate([lines[:inline], lines[inline:]], axis=1)
            planes = dot3(split(pair), ty, NN)
            for p in (0, 1):
                plane = planes[:, p * cross : (p + 1) * cross].reshape(n, kzs, cross)
                spot = (x * 2 + p) * kzs
                if kzs % 8 == 0:
                    send[phase][:, pl.ds(spot, kzs), :] = plane
                else:
                    for k in range(kzs):
                        send[phase][:, spot + k, :] = plane[:, k]

    def place_of(phase, j):
        block = counts[phase] * 2 * kzs
        return recv[phase].at[pl.ds(pl.multiple_of(j * block, block), block)]

    def exchange(phase, o, back):
        other = lax.rem(me + o, n)
        return pltpu.make_async_remote_copy(
            src_ref=send[phase].at[other],
            dst_ref=place_of(phase, lax.rem(me + n - o, n) if back else me),
            send_sem=all_send.at[phase, o],
            recv_sem=all_recv.at[phase, o],
            device_id=at(other),
            device_id_type=MESH,
        )

    def each(phase, act, back):
        def body(o, carry):
            getattr(exchange(phase, o, back), act)()
            return carry

        lax.fori_loop(1, n, body, 0)

    def launch(phase):
        transform(phase)
        each(phase, "start", False)
        place_of(phase, me)[...] = send[phase][me]

    for t in range(steps):
        amps = [amplitude(t, f) for f in (0, 1)]
        for f in (0, 1):
            if t == 0:
                for stage in stages[:3] if f == 0 else stages[3:]:
                    stage.wait()
            for r in range(2, rows - 2):
                advance(t, f, r, amps[f])
        if t == steps - 1 and phases > 1:
            shot_copy(0).start()
            shot_copy(0).wait_recv()
            launch(0)
        for f in (0, 1):
            for way, edge in ((1, (0, 1)), (0, (rows - 2, rows - 1))):
                halo_wait(t, way, f)
                for r in edge:
                    advance(t, f, r, amps[f])
                if t < steps - 1:
                    halo_send_do(t + 1, 1 - way, f, "start")
    shot_copy(phases - 1).start()
    bin_map = wbin[...]
    weight = jnp.zeros(bin_map.shape, F32)
    level = jnp.zeros(bin_map.shape, F32)
    for b in range(bins):
        hit = bin_map == b
        weight = jnp.where(hit, wweight[b], weight)
        level = jnp.where(hit, slevel[b], level)
    shot_copy(phases - 1).wait_recv()
    launch(phases - 1)

    first = 0
    for phase in range(phases):
        each(phase, "wait_recv", True)
        length = n * counts[phase]
        for k in range(kzs):
            for p in (0, 1):
                part = recv[phase][pl.ds(p * kzs + k, length, stride=2 * kzs), :]
                high, low = split(part)
                spot = (pl.ds(p * depth_len + first, length), pl.ds(k * cross, cross))
                xh[spot] = high
                xl[spot] = low
        first += length

    width = depth_len // ns
    full = dot3((txh[1 - s], txl[1 - s]), (xh[...], xl[...]), NN)
    for p in (0, 1):
        for k in range(kzs):
            swap_out[p, k] = full[p * width : (p + 1) * width, k * cross : (k + 1) * cross]
    swap = pltpu.make_async_remote_copy(
        src_ref=swap_out,
        dst_ref=swap_in,
        send_sem=swap_sems.at[0],
        recv_sem=swap_sems.at[1],
        device_id=(g, d, 1 - s),
        device_id_type=MESH,
    )
    swap.start()

    def shrink(real, imag, spot):
        real, imag = weight * real, weight * imag
        factor = 1.0 - level * lax.rsqrt(real * real + imag * imag + level * level)
        out_re[spot] = factor * real
        out_im[spot] = factor * imag

    full = dot3((txh[s], txl[s]), (xh[...], xl[...]), NN)
    for k in range(kzs):
        lanes = slice(k * cross, (k + 1) * cross)
        shrink(full[:width, lanes], full[width:, lanes], s * kzs + k)
    swap.wait_recv()
    for k in range(kzs):
        shrink(swap_in[0, k], swap_in[1, k], (1 - s) * kzs + k)

    for t in range(steps):
        for f in (0, 1):
            for way in (0, 1):
                halo_send_do(t, way, f, "wait_send")
    for phase in range(phases):
        shot_copy(phase).wait_send()
        each(phase, "wait_send", False)
    swap.wait_send()


def per_device(
    nd, ns,
    src_now, src_prev, rcv_now, rcv_prev, courant_sq, source_cells, shot_signs,
    source_wavelet, receiver_cells, receiver_data, wedge_bin, wedge_weight, shrink_level,
):
    _, rows, cross, inline = src_now.shape
    steps = source_wavelet.shape[0]
    n = nd * ns
    depth_len = rows * nd
    half = rows // ns
    kzs = inline // n
    counts = (half - 2, 2) if half == 4 and (4 * kzs) % 8 == 0 else (half,)
    order = np.concatenate(
        [
            np.array(
                [
                    j * rows + phase_start(counts, half, rows, phase, core) + i
                    for j in range(nd)
                    for core in range(ns)
                    for i in range(count)
                ]
            )
            for phase, count in enumerate(counts)
        ]
    )
    width = depth_len // ns
    c, s_ = dft_pair(inline)
    tz = halves(np.concatenate([c, -s_], axis=0))
    c, s_ = dft_pair(cross)
    ty = halves(np.block([[c, -s_], [s_, c]]))
    c, s_ = dft_pair(depth_len)
    c, s_ = c[:, order], s_[:, order]
    tx = halves(
        np.stack(
            [
                np.block(
                    [
                        [c[h * width : (h + 1) * width], s_[h * width : (h + 1) * width]],
                        [-s_[h * width : (h + 1) * width], c[h * width : (h + 1) * width]],
                    ]
                )
                for h in range(ns)
            ]
        )
    )
    vmem = pl.BlockSpec(memory_space=pltpu.VMEM)
    smem = pl.BlockSpec(memory_space=pltpu.SMEM)
    out = jax.ShapeDtypeStruct((inline // nd, width, cross), F32)
    dma = pltpu.SemaphoreType.DMA
    return pl.pallas_call(
        functools.partial(
            kernel, nd, ns, steps, rows, cross, inline, wedge_weight.shape[0],
            (depth_len, half, kzs, counts),
        ),
        out_shape=(out, out),
        in_specs=[pl.BlockSpec(memory_space=pl.ANY)] * 5 + [vmem] * 6 + [smem] * 2 + [vmem] * 6,
        out_specs=(vmem, vmem),
        scratch_shapes=[
            pltpu.VMEM((4, rows, cross, inline), F32),
            pltpu.VMEM((rows, cross, inline), F32),
            pltpu.VMEM((steps, 2, 2, 2, cross, inline), F32),
            pltpu.VMEM((steps, 2, rows, cross, inline), F32),
            pltpu.VMEM((rows, cross, inline), F32),
            pltpu.VMEM((2 * depth_len, kzs * cross), BF),
            pltpu.VMEM((2 * depth_len, kzs * cross), BF),
            pltpu.VMEM((2, kzs, width, cross), F32),
            pltpu.VMEM((2, kzs, width, cross), F32),
            dma((steps, 2, 2)),
            dma((steps, 2, 2)),
            dma((len(counts), 2)),
            dma((len(counts), n)),
            dma((len(counts), n)),
            dma((2,)),
            dma((5,)),
        ]
        + [pltpu.VMEM((c, cross, inline), F32) for c in counts]
        + [pltpu.VMEM((n, c * 2 * kzs, cross), F32) for c in counts]
        + [pltpu.VMEM((n * c * 2 * kzs, cross), F32) for c in counts],
        compiler_params=pltpu.CompilerParams(
            collective_id=0, has_side_effects=True, vmem_limit_bytes=56 * 1024 * 1024
        ),
    )(
        src_now, src_prev, rcv_now, rcv_prev, courant_sq,
        source_cells[None], shot_signs, source_wavelet, receiver_cells[None],
        jnp.transpose(receiver_data, (1, 0, 2)), wedge_bin, wedge_weight, shrink_level,
        *tz, *ty, *tx,
    )


def solution(mesh):
    return jax.shard_map(
        functools.partial(per_device, mesh.shape["depth"], mesh.shape["shot"]),
        mesh=mesh,
        in_specs=(
            P(("grp", "shot"), "depth", None, None),
            P(("grp", "shot"), "depth", None, None),
            P(("grp", "shot"), "depth", None, None),
            P(("grp", "shot"), "depth", None, None),
            P(("grp", "depth"), None, None),
            P(),
            P(("grp", "shot"), None),
            P(),
            P(),
            P(("grp", "shot"), None, None),
            P("shot", None),
            P(),
            P(),
        ),
        out_specs=(P(("grp", "depth"), "shot", None), P(("grp", "depth"), "shot", None)),
        check_vma=False,
    )
```

```python
import functools
import math

import jax
import jax.numpy as jnp
import numpy as np
from jax import lax
from jax.experimental import pallas as pl
from jax.experimental.pallas import tpu as pltpu
from jax.sharding import PartitionSpec as P

CENTER = -2.5
NEAR = 4.0 / 3.0
FAR = -1.0 / 12.0
MESH = pl.DeviceIdType.MESH
BF = jnp.bfloat16
F32 = jnp.float32


def dft_pair(length):
    index = np.arange(length)
    angle = (index[:, None] * index[None, :] % length) * (2.0 * math.pi / length)
    scale = 1.0 / math.sqrt(length)
    return np.cos(angle) * scale, np.sin(angle) * scale


def halves(table):
    table = table.astype(np.float32)
    high = table.astype(BF)
    low = (table - high.astype(np.float32)).astype(BF)
    return high, low


def split(value):
    high = value.astype(BF)
    return high, (value - high.astype(F32)).astype(BF)


def dot(a, b, dims):
    return lax.dot_general(a, b, (dims, ((), ())), preferred_element_type=F32)


def dot3(a, b, dims):
    (ah, al), (bh, bl) = a, b
    return dot(ah, bh, dims) + (dot(ah, bl, dims) + dot(al, bh, dims))


NN = ((1,), (0,))
NT = ((1,), (1,))


def phase_start(counts, half, rows, phase, core):
    if len(counts) == 1:
        return core * half
    if phase == 0:
        return 2 + core * (half - 2)
    return core * (rows - 2)


def kernel(
    nd, ns, steps, rows, cross, inline, bins, sizes,
    sn, sp, rn, rp, cs, scell, ssign, swave, rcell, rdata, wbin, wweight, slevel,
    tzh, tzl, tyh, tyl, txh, txl,
    out_re, out_im, out_weight, out_level, out_square,
    staged, courant, halo, waves, image, xh, xl, swap_out, swap_in,
    halo_send, halo_recv, shot_sems, all_send, all_recv, swap_sems, stage_sems,
    *buffers,
):
    depth_len, half, kzs, counts = sizes
    phases = len(counts)
    arrived, send, recv = (buffers[i * phases : (i + 1) * phases] for i in range(3))
    g, d, s = lax.axis_index("grp"), lax.axis_index("depth"), lax.axis_index("shot")
    n = nd * ns
    me = d * ns + s

    def rows_at(phase, core):
        return phase_start(counts, half, rows, phase, core)

    def at(j):
        return (g, j // ns, lax.rem(j, ns))

    stages = [
        pltpu.make_async_copy(src, dst, stage_sems.at[i])
        for i, (src, dst) in enumerate(
            [
                (sn.at[0], staged.at[0]),
                (sp.at[0], staged.at[1]),
                (cs, courant),
                (rn.at[0], staged.at[2]),
                (rp.at[0], staged.at[3]),
            ]
        )
    ]
    for stage in stages:
        stage.start()
    barrier = pltpu.get_barrier_semaphore()

    def greet(o, carry):
        pl.semaphore_signal(
            barrier, inc=1, device_id=at(lax.rem(me + o, n)), device_id_type=MESH
        )
        return carry

    lax.fori_loop(1, n, greet, 0)
    pl.semaphore_wait(barrier, n - 1)

    now = [[staged.at[0], staged.at[2]]] + [[waves.at[t, 0], waves.at[t, 1]] for t in range(steps)]
    before = [[staged.at[1], staged.at[3]]] + now
    outgoing = [[sn.at[0], rn.at[0]]] + now[1:]

    def halo_copy(t, way, f):
        rows_from = outgoing[t][f].at[pl.ds(0 if way == 0 else rows - 2, 2)]
        return pltpu.make_async_remote_copy(
            src_ref=rows_from,
            dst_ref=halo.at[t, way, f],
            send_sem=halo_send.at[t, way, f],
            recv_sem=halo_recv.at[t, way, f],
            device_id=(g, d - 1 if way == 0 else d + 1, s),
            device_id_type=MESH,
        )

    has = (d > 0, d < nd - 1)

    def halo_send_do(t, way, f, act):
        @pl.when(has[way])
        def _():
            getattr(halo_copy(t, way, f), act)()

    def halo_wait(t, way, f):
        @pl.when(has[1 - way])
        def _():
            halo_copy(t, way, f).wait_recv()

    for f in (0, 1):
        for way in (0, 1):
            halo_send_do(0, way, f, "start")

    for way in (0, 1):
        @pl.when(jnp.logical_not(has[1 - way]))
        def _():
            for t in range(steps):
                for f in (0, 1):
                    halo[t, way, f] = jnp.zeros((2, cross, inline), F32)

    row_iota = lax.broadcasted_iota(jnp.int32, (cross, 1), 0)
    lane = lax.broadcasted_iota(jnp.int32, (1, inline), 1)
    twice = lambda v: jnp.concatenate([v, v], axis=1)
    place = []
    for cells in (scell, rcell):
        c = twice(cells[...])
        depth_idx = c // (cross * inline)
        cross_idx = lax.rem(c // inline, cross)
        inline_idx = lax.rem(c, inline)
        on_y = row_iota == cross_idx
        zt = lax.broadcasted_iota(jnp.int32, (inline, 1), 0) == inline_idx
        place.append((depth_idx, on_y, jnp.where(zt, 1.0, 0.0).astype(BF)))
    signs = (2 * ssign[...] - 1).astype(F32)

    def amplitude(t, f):
        if f == 0:
            amp = signs * swave[pl.ds(t, 1), :]
        else:
            amp = rdata[steps - 1 - t]
        high = amp.astype(BF).astype(F32)
        return jnp.concatenate([high, amp - high], axis=1)

    def forcing(amp, f, r):
        depth_idx, on_y, zt = place[f]
        amp_row = jnp.where(depth_idx == d * rows + r, amp, 0.0)
        left = jnp.where(on_y, amp_row, 0.0).astype(BF)
        return dot(left, zt, NT)

    lane_coef = [
        (k, jnp.where((lane + k >= 0) & (lane + k < inline), c, 0.0))
        for k, c in ((1, NEAR), (-1, NEAR), (2, FAR), (-2, FAR))
    ]

    def move(u, k):
        zero = jnp.zeros((abs(k), inline), F32)
        if k > 0:
            return jnp.concatenate([u[k:], zero], axis=0)
        return jnp.concatenate([zero, u[:k]], axis=0)

    def advance(t, f, r, amp):
        field = now[t][f]

        def layer(q):
            if q < 0:
                return halo[t, 1, f, q + 2]
            if q >= rows:
                return halo[t, 0, f, q - rows]
            return field[q]

        u = layer(r)
        near = layer(r - 1) + layer(r + 1) + move(u, 1) + move(u, -1)
        far = layer(r - 2) + layer(r + 2) + move(u, 2) + move(u, -2)
        total = 3.0 * CENTER * u + NEAR * near + FAR * far
        for k, coef in lane_coef:
            total = total + coef * pltpu.roll(u, (-k) % inline, 1)
        new = 2.0 * u - before[t][f][r] + courant[r] * total + forcing(amp, f, r)
        if t < steps - 1 or f == 0:
            waves[t, f, r] = new
        if f == 1:
            product = waves[t, 0, r] * new
            if t == 0:
                image[r] = product
            else:
                image[r] = image[r] + product

    def shot_copy(phase):
        return pltpu.make_async_remote_copy(
            src_ref=image.at[pl.ds(rows_at(phase, 1 - s), counts[phase])],
            dst_ref=arrived[phase],
            send_sem=shot_sems.at[phase, 0],
            recv_sem=shot_sems.at[phase, 1],
            device_id=(g, d, 1 - s),
            device_id_type=MESH,
        )

    tz = (tzh[...], tzl[...])
    ty = (tyh[...], tyl[...])

    def transform(phase):
        mine = rows_at(phase, s)
        for x in range(counts[phase]):
            summed = image[mine + x] + arrived[phase][x]
            lines = dot3(tz, split(summed), NT)
            pair = jnp.concatenate([lines[:inline], lines[inline:]], axis=1)
            planes = dot3(split(pair), ty, NN)
            for p in (0, 1):
                plane = planes[:, p * cross : (p + 1) * cross].reshape(n, kzs, cross)
                spot = (x * 2 + p) * kzs
                if kzs % 8 == 0:
                    send[phase][:, pl.ds(spot, kzs), :] = plane
                else:
                    for k in range(kzs):
                        send[phase][:, spot + k, :] = plane[:, k]

    def place_of(phase, j):
        block = counts[phase] * 2 * kzs
        return recv[phase].at[pl.ds(pl.multiple_of(j * block, block), block)]

    def exchange(phase, o, back):
        other = lax.rem(me + o, n)
        return pltpu.make_async_remote_copy(
            src_ref=send[phase].at[other],
            dst_ref=place_of(phase, lax.rem(me + n - o, n) if back else me),
            send_sem=all_send.at[phase, o],
            recv_sem=all_recv.at[phase, o],
            device_id=at(other),
            device_id_type=MESH,
        )

    def each(phase, act, back):
        def body(o, carry):
            getattr(exchange(phase, o, back), act)()
            return carry

        lax.fori_loop(1, n, body, 0)

    def launch(phase):
        transform(phase)
        each(phase, "start", False)
        place_of(phase, me)[...] = send[phase][me]

    for t in range(steps):
        amps = [amplitude(t, f) for f in (0, 1)]
        for f in (0, 1):
            if t == 0:
                for stage in stages[:3] if f == 0 else stages[3:]:
                    stage.wait()
            for r in range(2, rows - 2):
                advance(t, f, r, amps[f])
        if t == steps - 1 and phases > 1:
            shot_copy(0).start()
            shot_copy(0).wait_recv()
            launch(0)
        for f in (0, 1):
            for way, edge in ((1, (0, 1)), (0, (rows - 2, rows - 1))):
                halo_wait(t, way, f)
                for r in edge:
                    advance(t, f, r, amps[f])
                if t < steps - 1:
                    halo_send_do(t + 1, 1 - way, f, "start")
    shot_copy(phases - 1).start()
    bin_map = wbin[...]
    weight = jnp.zeros(bin_map.shape, F32)
    level = jnp.zeros(bin_map.shape, F32)
    for b in range(bins):
        hit = bin_map == b
        weight = jnp.where(hit, wweight[b], weight)
        level = jnp.where(hit, slevel[b], level)
    out_weight[...] = weight
    out_level[...] = level
    out_square[...] = level * level
    shot_copy(phases - 1).wait_recv()
    launch(phases - 1)

    first = 0
    for phase in range(phases):
        each(phase, "wait_recv", True)
        length = n * counts[phase]
        for k in range(kzs):
            for p in (0, 1):
                part = recv[phase][pl.ds(p * kzs + k, length, stride=2 * kzs), :]
                high, low = split(part)
                spot = (pl.ds(p * depth_len + first, length), pl.ds(k * cross, cross))
                xh[spot] = high
                xl[spot] = low
        first += length

    width = depth_len // ns
    full = dot3((txh[1 - s], txl[1 - s]), (xh[...], xl[...]), NN)
    for p in (0, 1):
        for k in range(kzs):
            swap_out[p, k] = full[p * width : (p + 1) * width, k * cross : (k + 1) * cross]
    swap = pltpu.make_async_remote_copy(
        src_ref=swap_out,
        dst_ref=swap_in,
        send_sem=swap_sems.at[0],
        recv_sem=swap_sems.at[1],
        device_id=(g, d, 1 - s),
        device_id_type=MESH,
    )
    swap.start()

    def store(real, imag, spot):
        out_re[spot] = real
        out_im[spot] = imag

    full = dot3((txh[s], txl[s]), (xh[...], xl[...]), NN)
    for k in range(kzs):
        lanes = slice(k * cross, (k + 1) * cross)
        store(full[:width, lanes], full[width:, lanes], s * kzs + k)
    swap.wait_recv()
    for k in range(kzs):
        store(swap_in[0, k], swap_in[1, k], (1 - s) * kzs + k)

    for t in range(steps):
        for f in (0, 1):
            for way in (0, 1):
                halo_send_do(t, way, f, "wait_send")
    for phase in range(phases):
        shot_copy(phase).wait_send()
        each(phase, "wait_send", False)
    swap.wait_send()


def per_device(
    nd, ns,
    src_now, src_prev, rcv_now, rcv_prev, courant_sq, source_cells, shot_signs,
    source_wavelet, receiver_cells, receiver_data, wedge_bin, wedge_weight, shrink_level,
):
    _, rows, cross, inline = src_now.shape
    steps = source_wavelet.shape[0]
    n = nd * ns
    depth_len = rows * nd
    half = rows // ns
    kzs = inline // n
    counts = (half - 2, 2) if half == 4 and (4 * kzs) % 8 == 0 else (half,)
    order = np.concatenate(
        [
            np.array(
                [
                    j * rows + phase_start(counts, half, rows, phase, core) + i
                    for j in range(nd)
                    for core in range(ns)
                    for i in range(count)
                ]
            )
            for phase, count in enumerate(counts)
        ]
    )
    width = depth_len // ns
    c, s_ = dft_pair(inline)
    tz = halves(np.concatenate([c, -s_], axis=0))
    c, s_ = dft_pair(cross)
    ty = halves(np.block([[c, -s_], [s_, c]]))
    c, s_ = dft_pair(depth_len)
    c, s_ = c[:, order], s_[:, order]
    tx = halves(
        np.stack(
            [
                np.block(
                    [
                        [c[h * width : (h + 1) * width], s_[h * width : (h + 1) * width]],
                        [-s_[h * width : (h + 1) * width], c[h * width : (h + 1) * width]],
                    ]
                )
                for h in range(ns)
            ]
        )
    )
    vmem = pl.BlockSpec(memory_space=pltpu.VMEM)
    smem = pl.BlockSpec(memory_space=pltpu.SMEM)
    out = jax.ShapeDtypeStruct((inline // nd, width, cross), F32)
    dma = pltpu.SemaphoreType.DMA
    table = jax.ShapeDtypeStruct((width, cross), F32)
    real, imag, weight, level, square = pl.pallas_call(
        functools.partial(
            kernel, nd, ns, steps, rows, cross, inline, wedge_weight.shape[0],
            (depth_len, half, kzs, counts),
        ),
        out_shape=(out, out, table, table, table),
        in_specs=[pl.BlockSpec(memory_space=pl.ANY)] * 5 + [vmem] * 6 + [smem] * 2 + [vmem] * 6,
        out_specs=(vmem,) * 5,
        scratch_shapes=[
            pltpu.VMEM((4, rows, cross, inline), F32),
            pltpu.VMEM((rows, cross, inline), F32),
            pltpu.VMEM((steps, 2, 2, 2, cross, inline), F32),
            pltpu.VMEM((steps, 2, rows, cross, inline), F32),
            pltpu.VMEM((rows, cross, inline), F32),
            pltpu.VMEM((2 * depth_len, kzs * cross), BF),
            pltpu.VMEM((2 * depth_len, kzs * cross), BF),
            pltpu.VMEM((2, kzs, width, cross), F32),
            pltpu.VMEM((2, kzs, width, cross), F32),
            dma((steps, 2, 2)),
            dma((steps, 2, 2)),
            dma((len(counts), 2)),
            dma((len(counts), n)),
            dma((len(counts), n)),
            dma((2,)),
            dma((5,)),
        ]
        + [pltpu.VMEM((c, cross, inline), F32) for c in counts]
        + [pltpu.VMEM((n, c * 2 * kzs, cross), F32) for c in counts]
        + [pltpu.VMEM((n * c * 2 * kzs, cross), F32) for c in counts],
        compiler_params=pltpu.CompilerParams(
            collective_id=0, has_side_effects=True, vmem_limit_bytes=56 * 1024 * 1024
        ),
    )(
        src_now, src_prev, rcv_now, rcv_prev, courant_sq,
        source_cells[None], shot_signs, source_wavelet, receiver_cells[None],
        jnp.transpose(receiver_data, (1, 0, 2)), wedge_bin, wedge_weight, shrink_level,
        *tz, *ty, *tx,
    )
    real, imag = weight[None] * real, weight[None] * imag
    factor = 1.0 - level[None] * lax.rsqrt(real * real + imag * imag + square[None])
    return factor * real, factor * imag


def solution(mesh):
    return jax.shard_map(
        functools.partial(per_device, mesh.shape["depth"], mesh.shape["shot"]),
        mesh=mesh,
        in_specs=(
            P(("grp", "shot"), "depth", None, None),
            P(("grp", "shot"), "depth", None, None),
            P(("grp", "shot"), "depth", None, None),
            P(("grp", "shot"), "depth", None, None),
            P(("grp", "depth"), None, None),
            P(),
            P(("grp", "shot"), None),
            P(),
            P(),
            P(("grp", "shot"), None, None),
            P("shot", None),
            P(),
            P(),
        ),
        out_specs=(P(("grp", "depth"), "shot", None), P(("grp", "depth"), "shot", None)),
        check_vma=False,
    )
```

```python
import functools
import math

import jax
import jax.numpy as jnp
import numpy as np
from jax import lax
from jax.experimental import pallas as pl
from jax.experimental.pallas import tpu as pltpu
from jax.sharding import PartitionSpec as P

CENTER = -2.5
NEAR = 4.0 / 3.0
FAR = -1.0 / 12.0
MESH = pl.DeviceIdType.MESH
BF = jnp.bfloat16
F32 = jnp.float32


def dft_pair(length):
    index = np.arange(length)
    angle = (index[:, None] * index[None, :] % length) * (2.0 * math.pi / length)
    scale = 1.0 / math.sqrt(length)
    return np.cos(angle) * scale, np.sin(angle) * scale


def halves(table):
    table = table.astype(np.float32)
    high = table.astype(BF)
    low = (table - high.astype(np.float32)).astype(BF)
    return high, low


def split(value):
    high = value.astype(BF)
    return high, (value - high.astype(F32)).astype(BF)


def dot(a, b, dims):
    return lax.dot_general(a, b, (dims, ((), ())), preferred_element_type=F32)


def dot3(a, b, dims):
    (ah, al), (bh, bl) = a, b
    return dot(ah, bh, dims) + (dot(ah, bl, dims) + dot(al, bh, dims))


NN = ((1,), (0,))
NT = ((1,), (1,))


def phase_start(counts, half, rows, phase, core):
    if len(counts) == 1:
        return core * half
    if phase == 0:
        return 2 + core * (half - 2)
    return core * (rows - 2)


def kernel(
    nd, ns, steps, rows, cross, inline, bins, sizes,
    sn, sp, rn, rp, cs, scell, ssign, swave, rcell, rdata, wbin, wweight, slevel,
    tzh, tzl, tyh, tyl, txh, txl,
    out_re, out_im, out_weight, out_level, out_square,
    staged, courant, halo, waves, image, xh, xl, swap_out, swap_in,
    halo_send, halo_recv, shot_sems, all_send, all_recv, swap_sems, stage_sems,
    *buffers,
):
    depth_len, half, kzs, counts = sizes
    phases = len(counts)
    arrived, send, recv = (buffers[i * phases : (i + 1) * phases] for i in range(3))
    g, d, s = lax.axis_index("grp"), lax.axis_index("depth"), lax.axis_index("shot")
    n = nd * ns
    me = d * ns + s

    def rows_at(phase, core):
        return phase_start(counts, half, rows, phase, core)

    def at(j):
        return (g, j // ns, lax.rem(j, ns))

    stages = [
        pltpu.make_async_copy(src, dst, stage_sems.at[i])
        for i, (src, dst) in enumerate(
            [
                (sn.at[0], staged.at[0]),
                (sp.at[0], staged.at[1]),
                (cs, courant),
                (rn.at[0], staged.at[2]),
                (rp.at[0], staged.at[3]),
            ]
        )
    ]
    for stage in stages:
        stage.start()
    barrier = pltpu.get_barrier_semaphore()

    def greet(o, carry):
        pl.semaphore_signal(
            barrier, inc=1, device_id=at(lax.rem(me + o, n)), device_id_type=MESH
        )
        return carry

    lax.fori_loop(1, n, greet, 0)
    pl.semaphore_wait(barrier, n - 1)

    now = [[staged.at[0], staged.at[2]]] + [[waves.at[t, 0], waves.at[t, 1]] for t in range(steps)]
    before = [[staged.at[1], staged.at[3]]] + now
    outgoing = [[sn.at[0], rn.at[0]]] + now[1:]

    def halo_copy(t, way, f):
        rows_from = outgoing[t][f].at[pl.ds(0 if way == 0 else rows - 2, 2)]
        return pltpu.make_async_remote_copy(
            src_ref=rows_from,
            dst_ref=halo.at[t, way, f],
            send_sem=halo_send.at[t, way, f],
            recv_sem=halo_recv.at[t, way, f],
            device_id=(g, d - 1 if way == 0 else d + 1, s),
            device_id_type=MESH,
        )

    has = (d > 0, d < nd - 1)

    def halo_send_do(t, way, f, act):
        @pl.when(has[way])
        def _():
            getattr(halo_copy(t, way, f), act)()

    def halo_wait(t, way, f):
        @pl.when(has[1 - way])
        def _():
            halo_copy(t, way, f).wait_recv()

    for f in (0, 1):
        for way in (0, 1):
            halo_send_do(0, way, f, "start")

    for way in (0, 1):
        @pl.when(jnp.logical_not(has[1 - way]))
        def _():
            for t in range(steps):
                for f in (0, 1):
                    halo[t, way, f] = jnp.zeros((2, cross, inline), F32)

    row_iota = lax.broadcasted_iota(jnp.int32, (cross, 1), 0)
    lane = lax.broadcasted_iota(jnp.int32, (1, inline), 1)
    twice = lambda v: jnp.concatenate([v, v], axis=1)
    place = []
    for cells in (scell, rcell):
        c = twice(cells[...])
        depth_idx = c // (cross * inline)
        cross_idx = lax.rem(c // inline, cross)
        inline_idx = lax.rem(c, inline)
        on_y = row_iota == cross_idx
        zt = lax.broadcasted_iota(jnp.int32, (inline, 1), 0) == inline_idx
        place.append((depth_idx, on_y, jnp.where(zt, 1.0, 0.0).astype(BF)))
    signs = (2 * ssign[...] - 1).astype(F32)

    def amplitude(t, f):
        if f == 0:
            amp = signs * swave[pl.ds(t, 1), :]
        else:
            amp = rdata[steps - 1 - t]
        high = amp.astype(BF).astype(F32)
        return jnp.concatenate([high, amp - high], axis=1)

    def forcing(amp, f, r):
        depth_idx, on_y, zt = place[f]
        amp_row = jnp.where(depth_idx == d * rows + r, amp, 0.0)
        left = jnp.where(on_y, amp_row, 0.0).astype(BF)
        return dot(left, zt, NT)

    lane_coef = [
        (k, jnp.where((lane + k >= 0) & (lane + k < inline), c, 0.0))
        for k, c in ((1, NEAR), (-1, NEAR), (2, FAR), (-2, FAR))
    ]

    def move(u, k):
        zero = jnp.zeros((abs(k), inline), F32)
        if k > 0:
            return jnp.concatenate([u[k:], zero], axis=0)
        return jnp.concatenate([zero, u[:k]], axis=0)

    def advance(t, f, r, amp):
        field = now[t][f]

        def layer(q):
            if q < 0:
                return halo[t, 1, f, q + 2]
            if q >= rows:
                return halo[t, 0, f, q - rows]
            return field[q]

        u = layer(r)
        near = layer(r - 1) + layer(r + 1) + move(u, 1) + move(u, -1)
        far = layer(r - 2) + layer(r + 2) + move(u, 2) + move(u, -2)
        total = 3.0 * CENTER * u + NEAR * near + FAR * far
        for k, coef in lane_coef:
            total = total + coef * pltpu.roll(u, (-k) % inline, 1)
        new = 2.0 * u - before[t][f][r] + courant[r] * total + forcing(amp, f, r)
        if t < steps - 1 or f == 0:
            waves[t, f, r] = new
        if f == 1:
            product = waves[t, 0, r] * new
            if t == 0:
                image[r] = product
            else:
                image[r] = image[r] + product

    def shot_copy(phase):
        return pltpu.make_async_remote_copy(
            src_ref=image.at[pl.ds(rows_at(phase, 1 - s), counts[phase])],
            dst_ref=arrived[phase],
            send_sem=shot_sems.at[phase, 0],
            recv_sem=shot_sems.at[phase, 1],
            device_id=(g, d, 1 - s),
            device_id_type=MESH,
        )

    tz = (tzh[...], tzl[...])
    ty = (tyh[...], tyl[...])

    def transform(phase):
        mine = rows_at(phase, s)
        for x in range(counts[phase]):
            summed = image[mine + x] + arrived[phase][x]
            lines = dot3(tz, split(summed), NT)
            pair = jnp.concatenate([lines[:inline], lines[inline:]], axis=1)
            planes = dot3(split(pair), ty, NN)
            for p in (0, 1):
                plane = planes[:, p * cross : (p + 1) * cross].reshape(n, kzs, cross)
                spot = (x * 2 + p) * kzs
                if kzs % 8 == 0:
                    send[phase][:, pl.ds(spot, kzs), :] = plane
                else:
                    for k in range(kzs):
                        send[phase][:, spot + k, :] = plane[:, k]

    def place_of(phase, j):
        block = counts[phase] * 2 * kzs
        return recv[phase].at[pl.ds(pl.multiple_of(j * block, block), block)]

    def exchange(phase, o, back):
        other = lax.rem(me + o, n)
        return pltpu.make_async_remote_copy(
            src_ref=send[phase].at[other],
            dst_ref=place_of(phase, lax.rem(me + n - o, n) if back else me),
            send_sem=all_send.at[phase, o],
            recv_sem=all_recv.at[phase, o],
            device_id=at(other),
            device_id_type=MESH,
        )

    def each(phase, act, back):
        def body(o, carry):
            getattr(exchange(phase, o, back), act)()
            return carry

        lax.fori_loop(1, n, body, 0)

    def launch(phase):
        transform(phase)
        each(phase, "start", False)
        place_of(phase, me)[...] = send[phase][me]

    for t in range(steps):
        amps = [amplitude(t, f) for f in (0, 1)]
        for f in (0, 1):
            if t == 0:
                for stage in stages[:3] if f == 0 else stages[3:]:
                    stage.wait()
            for r in range(2, rows - 2):
                advance(t, f, r, amps[f])
        if t == steps - 1 and phases > 1:
            shot_copy(0).start()
            shot_copy(0).wait_recv()
            launch(0)
        for way, edge in ((1, (0, 1)), (0, (rows - 2, rows - 1))):
            for f in (0, 1):
                halo_wait(t, way, f)
                for r in edge:
                    advance(t, f, r, amps[f])
                if t < steps - 1:
                    halo_send_do(t + 1, 1 - way, f, "start")
    shot_copy(phases - 1).start()
    bin_map = wbin[...]
    weight = jnp.zeros(bin_map.shape, F32)
    level = jnp.zeros(bin_map.shape, F32)
    for b in range(bins):
        hit = bin_map == b
        weight = jnp.where(hit, wweight[b], weight)
        level = jnp.where(hit, slevel[b], level)
    out_weight[...] = weight
    out_level[...] = level
    out_square[...] = level * level
    shot_copy(phases - 1).wait_recv()
    launch(phases - 1)

    first = 0
    for phase in range(phases):
        each(phase, "wait_recv", True)
        length = n * counts[phase]
        for k in range(kzs):
            for p in (0, 1):
                part = recv[phase][pl.ds(p * kzs + k, length, stride=2 * kzs), :]
                high, low = split(part)
                spot = (pl.ds(p * depth_len + first, length), pl.ds(k * cross, cross))
                xh[spot] = high
                xl[spot] = low
        first += length

    width = depth_len // ns
    full = dot3((txh[1 - s], txl[1 - s]), (xh[...], xl[...]), NN)
    for p in (0, 1):
        for k in range(kzs):
            swap_out[p, k] = full[p * width : (p + 1) * width, k * cross : (k + 1) * cross]
    swap = pltpu.make_async_remote_copy(
        src_ref=swap_out,
        dst_ref=swap_in,
        send_sem=swap_sems.at[0],
        recv_sem=swap_sems.at[1],
        device_id=(g, d, 1 - s),
        device_id_type=MESH,
    )
    swap.start()

    def store(real, imag, spot):
        out_re[spot] = real
        out_im[spot] = imag

    full = dot3((txh[s], txl[s]), (xh[...], xl[...]), NN)
    for k in range(kzs):
        lanes = slice(k * cross, (k + 1) * cross)
        store(full[:width, lanes], full[width:, lanes], s * kzs + k)
    swap.wait_recv()
    for k in range(kzs):
        store(swap_in[0, k], swap_in[1, k], (1 - s) * kzs + k)

    for t in range(steps):
        for f in (0, 1):
            for way in (0, 1):
                halo_send_do(t, way, f, "wait_send")
    for phase in range(phases):
        shot_copy(phase).wait_send()
        each(phase, "wait_send", False)
    swap.wait_send()


def per_device(
    nd, ns,
    src_now, src_prev, rcv_now, rcv_prev, courant_sq, source_cells, shot_signs,
    source_wavelet, receiver_cells, receiver_data, wedge_bin, wedge_weight, shrink_level,
):
    _, rows, cross, inline = src_now.shape
    steps = source_wavelet.shape[0]
    n = nd * ns
    depth_len = rows * nd
    half = rows // ns
    kzs = inline // n
    counts = (half - 2, 2) if half == 4 and (4 * kzs) % 8 == 0 else (half,)
    order = np.concatenate(
        [
            np.array(
                [
                    j * rows + phase_start(counts, half, rows, phase, core) + i
                    for j in range(nd)
                    for core in range(ns)
                    for i in range(count)
                ]
            )
            for phase, count in enumerate(counts)
        ]
    )
    width = depth_len // ns
    c, s_ = dft_pair(inline)
    tz = halves(np.concatenate([c, -s_], axis=0))
    c, s_ = dft_pair(cross)
    ty = halves(np.block([[c, -s_], [s_, c]]))
    c, s_ = dft_pair(depth_len)
    c, s_ = c[:, order], s_[:, order]
    tx = halves(
        np.stack(
            [
                np.block(
                    [
                        [c[h * width : (h + 1) * width], s_[h * width : (h + 1) * width]],
                        [-s_[h * width : (h + 1) * width], c[h * width : (h + 1) * width]],
                    ]
                )
                for h in range(ns)
            ]
        )
    )
    vmem = pl.BlockSpec(memory_space=pltpu.VMEM)
    smem = pl.BlockSpec(memory_space=pltpu.SMEM)
    out = jax.ShapeDtypeStruct((inline // nd, width, cross), F32)
    dma = pltpu.SemaphoreType.DMA
    table = jax.ShapeDtypeStruct((width, cross), F32)
    real, imag, weight, level, square = pl.pallas_call(
        functools.partial(
            kernel, nd, ns, steps, rows, cross, inline, wedge_weight.shape[0],
            (depth_len, half, kzs, counts),
        ),
        out_shape=(out, out, table, table, table),
        in_specs=[pl.BlockSpec(memory_space=pl.ANY)] * 5 + [vmem] * 6 + [smem] * 2 + [vmem] * 6,
        out_specs=(vmem,) * 5,
        scratch_shapes=[
            pltpu.VMEM((4, rows, cross, inline), F32),
            pltpu.VMEM((rows, cross, inline), F32),
            pltpu.VMEM((steps, 2, 2, 2, cross, inline), F32),
            pltpu.VMEM((steps, 2, rows, cross, inline), F32),
            pltpu.VMEM((rows, cross, inline), F32),
            pltpu.VMEM((2 * depth_len, kzs * cross), BF),
            pltpu.VMEM((2 * depth_len, kzs * cross), BF),
            pltpu.VMEM((2, kzs, width, cross), F32),
            pltpu.VMEM((2, kzs, width, cross), F32),
            dma((steps, 2, 2)),
            dma((steps, 2, 2)),
            dma((len(counts), 2)),
            dma((len(counts), n)),
            dma((len(counts), n)),
            dma((2,)),
            dma((5,)),
        ]
        + [pltpu.VMEM((c, cross, inline), F32) for c in counts]
        + [pltpu.VMEM((n, c * 2 * kzs, cross), F32) for c in counts]
        + [pltpu.VMEM((n * c * 2 * kzs, cross), F32) for c in counts],
        compiler_params=pltpu.CompilerParams(
            collective_id=0, has_side_effects=True, vmem_limit_bytes=56 * 1024 * 1024
        ),
    )(
        src_now, src_prev, rcv_now, rcv_prev, courant_sq,
        source_cells[None], shot_signs, source_wavelet, receiver_cells[None],
        jnp.transpose(receiver_data, (1, 0, 2)), wedge_bin, wedge_weight, shrink_level,
        *tz, *ty, *tx,
    )
    real, imag = weight[None] * real, weight[None] * imag
    factor = 1.0 - level[None] * lax.rsqrt(real * real + imag * imag + square[None])
    return factor * real, factor * imag


def solution(mesh):
    return jax.shard_map(
        functools.partial(per_device, mesh.shape["depth"], mesh.shape["shot"]),
        mesh=mesh,
        in_specs=(
            P(("grp", "shot"), "depth", None, None),
            P(("grp", "shot"), "depth", None, None),
            P(("grp", "shot"), "depth", None, None),
            P(("grp", "shot"), "depth", None, None),
            P(("grp", "depth"), None, None),
            P(),
            P(("grp", "shot"), None),
            P(),
            P(),
            P(("grp", "shot"), None, None),
            P("shot", None),
            P(),
            P(),
        ),
        out_specs=(P(("grp", "depth"), "shot", None), P(("grp", "depth"), "shot", None)),
        check_vma=False,
    )
```
